256 devices in a mesh: seq: 32 (over z, x), head: 8 (over y, core).
Axes of the slice: x: 4, y: 4, z: 8, core: 2. Of those that a mesh axis runs over, the one named last changes fastest.
Arguments:
- queries: bfloat16 [16, 16384, 128], P(None, ('seq', 'head')), may hold values from -0.5390625 to 0.5390625
- keys: bfloat16 [16, 16384, 128], P(None, ('seq', 'head')), may hold values from -0.5390625 to 0.5390625
- values: bfloat16 [16, 16384, 128], P(None, ('seq', 'head')), may hold values from -24 to 24
- out_grad: bfloat16 [16, 16384, 128], P(None, ('seq', 'head')), may hold values from -6 to 6
- regular: float32 [16, 128], P('head'), may hold values from 0.25 to 4
Outputs:
- output: bfloat16 [16, 16384, 128], P(None, ('seq', 'head'))
- query_grad: bfloat16 [16, 16384, 128], P(None, ('seq', 'head'))
- key_grad: bfloat16 [16, 16384, 128], P(None, ('seq', 'head'))
- value_grad: bfloat16 [16, 16384, 128], P(None, ('seq', 'head'))
The draws below stay inside these ranges and needn't reach their ends.
All inputs are finite; a program needn't handle non-finite values.
Results may differ from the reference program's by a relative error of at most 0.001.
Values may be sent and summed in bfloat16 or wider, within the bound.
No kernel may reach another device: no remote copies, remote signals or barrier semaphores. Data moves between devices by JAX's collectives and lax.ppermute only.
A program may use at most 64 MiB of HBM per device.

```python
import math
from functools import partial
import jax
import jax.numpy as jnp
from jax import lax

HEADS = 16
DH = 128
GROUP = 128
TOKENS = 16384


def levels(key, shape, split, smallest, high):
    def one(dim, parts):
        heights = jax.random.uniform(jax.random.fold_in(jax.random.fold_in(key, 6), dim), (parts,), jnp.float32, smallest / len(split), high / len(split))
        return jnp.repeat(jnp.exp(heights), shape[dim] // parts).reshape((-1,) + (1,) * (len(shape) - dim - 1))

    factor_of = one(*split[0])
    for cut in split[1:]:
        factor_of = factor_of * one(*cut)
    return factor_of


def bell_draw(own_key, dims, spread, bound, shards=(), kind=jnp.bfloat16):
    level = levels(own_key, dims, shards, -0.22, 0.18) if shards else 1.0
    values = jax.random.normal(own_key, dims, jnp.float32) * spread * level
    return jnp.minimum(jnp.maximum(values, -bound), bound).astype(kind)


def setup_inputs(seed: int = 0) -> dict:
    key_list = jax.random.split(jax.random.key(seed), 6)
    return {
        "queries": bell_draw(key_list[0], (HEADS, TOKENS, DH), 0.09, 0.5390625, ((1, 256),)),
        "keys": bell_draw(key_list[1], (HEADS, TOKENS, DH), 0.09, 0.5390625, ((1, 256),)),
        "values": bell_draw(key_list[2], (HEADS, TOKENS, DH), 4.0, 24.0, ((1, 256),)),
        "out_grad": bell_draw(key_list[3], (HEADS, TOKENS, DH), 1.0, 6.0, ((1, 256),)),
        "regular": jnp.clip(jnp.exp(math.log(4.0) - 2.7725887 * jax.random.uniform(key_list[4], (HEADS, DH), jnp.float32) ** levels(key_list[4], (HEADS, DH), ((0, 8),), -0.2, 0.2)), 0.25, 4.0),
    }


def exact_einsum(form, left, right):
    return jnp.einsum(form, left, right, precision=lax.Precision.HIGHEST)

def group_output(query_rows, key_rows, value_rows, gram_in, state_in, causal):
    eye_dim = jnp.broadcast_to(jnp.eye(gram_in.shape[-1], dtype=jnp.float32), gram_in.shape)
    low_gram = jnp.linalg.cholesky(gram_in)
    half_inv = lax.linalg.triangular_solve(low_gram, eye_dim, left_side=True, lower=True)
    inverse = lax.linalg.triangular_solve(low_gram, half_inv, left_side=True, lower=True, transpose_a=True)
    key_inv = exact_einsum('...cd,...de->...ce', key_rows, inverse)
    inner_mat = exact_einsum('...ce,...te->...ct', key_inv, key_rows)
    eye_rows = jnp.eye(causal.shape[0], dtype=jnp.float32)
    low_mix = jnp.linalg.cholesky(inner_mat + eye_rows)
    right_side = exact_einsum('...ce,...te->...ct', key_inv, query_rows)
    first_pass = lax.linalg.triangular_solve(low_mix, right_side, left_side=True, lower=True) * causal
    second_pass = lax.linalg.triangular_solve(low_mix, first_pass, left_side=True, lower=True, transpose_a=True) * causal
    solved = exact_einsum('...de,...te->...dt', inverse, query_rows) - exact_einsum('...cd,...ct->...dt', key_inv, second_pass)
    scores = exact_einsum('...cd,...dt->...ct', key_rows, solved) * causal
    return exact_einsum('...ed,...dt->...te', state_in, solved) + exact_einsum('...ce,...ct->...te', value_rows, scores)

def reference(queries, keys, values, out_grad, regular):
    block_count = TOKENS // GROUP
    positions = jnp.arange(GROUP)
    causal = (positions[:, None] <= positions[None, :]).astype(jnp.float32)

    def blocks(array):
        return array.astype(jnp.float32).reshape(HEADS, block_count, GROUP, DH).transpose(1, 0, 2, 3)
    query_all, key_all, value_all, grad_all = (blocks(queries), blocks(keys), blocks(values), blocks(out_grad))
    base = regular.astype(jnp.float32)[:, :, None] * jnp.eye(DH, dtype=jnp.float32)
    zero_state = jnp.zeros((HEADS, DH, DH), jnp.float32)

    def forward(carried, inputs_now):
        gram_sum, state_sum = carried
        query_rows, key_rows, value_rows, grad_rows = inputs_now
        result, pull = jax.vjp(partial(group_output, causal=causal), query_rows, key_rows, value_rows, base + gram_sum, state_sum)
        grads = pull(grad_rows)
        gram_next = gram_sum + exact_einsum('hcd,hce->hde', key_rows, key_rows)
        state_next = state_sum + exact_einsum('hce,hcd->hed', value_rows, key_rows)
        return ((gram_next, state_next), (result,) + tuple(grads))
    unused, (result, dq_part, dk_part, dv_part, dgram_part, dstate_part) = lax.scan(forward, (zero_state, zero_state), (query_all, key_all, value_all, grad_all))

    def backward(carried, inputs_now):
        gram_after, state_after = carried
        key_rows, value_rows, dk_rows, dv_rows, dgram_rows, dstate_rows = inputs_now
        sym_after = gram_after + jnp.swapaxes(gram_after, -1, -2)
        dk_full = dk_rows + exact_einsum('hde,hce->hcd', sym_after, key_rows) + exact_einsum('hed,hce->hcd', state_after, value_rows)
        dv_full = dv_rows + exact_einsum('hed,hcd->hce', state_after, key_rows)
        return ((gram_after + dgram_rows, state_after + dstate_rows), (dk_full, dv_full))
    unused_back, (dk_total, dv_total) = lax.scan(backward, (zero_state, zero_state), (key_all, value_all, dk_part, dv_part, dgram_part, dstate_part), reverse=True)

    def unblock(array):
        return array.transpose(1, 0, 2, 3).reshape(HEADS, TOKENS, DH).astype(jnp.bfloat16)
    return (unblock(result), unblock(dq_part), unblock(dk_total), unblock(dv_total))
```

```python
import jax
import jax.numpy as jnp
from jax import lax
from jax.experimental import pallas as pl
from jax.experimental.pallas import tpu as pltpu
from jax.sharding import PartitionSpec as P

F32 = jnp.float32
BF16 = jnp.bfloat16
BLOCK = 128
DIM = 128
TILE = 8
PARAMS = pltpu.CompilerParams(vmem_limit_bytes=56 * 1024 * 1024)


def halves(x):
    high = x.astype(BF16)
    return high, (x - high.astype(F32)).astype(BF16)


def thirds(x):
    high = x.astype(BF16)
    rest = x - high.astype(F32)
    mid = rest.astype(BF16)
    return high, mid, (rest - mid.astype(F32)).astype(BF16)


def contract(pairs, left_dim, right_dim):
    left = [a for a, _ in pairs]
    right = [b for _, b in pairs]
    left = left[0] if len(left) == 1 else jnp.concatenate(left, axis=left_dim)
    right = right[0] if len(right) == 1 else jnp.concatenate(right, axis=right_dim)
    return lax.dot_general(
        left, right, (((left_dim,), (right_dim,)), ((), ())), preferred_element_type=F32
    )


def cross(left, right):
    return [(left[0], right[0]), (left[0], right[1]), (left[1], right[0])]


def owned_rows(ref, block, which):
    first = 2 * block
    second = first + 1
    return jnp.concatenate(
        [
            ref[2 * (first % 8) + first // 8, which],
            ref[2 * (second % 8) + second // 8, which],
        ],
        axis=0,
    )


def put_rows(ref, block, which, rows):
    half = BLOCK // 2
    first = 2 * block
    second = first + 1
    ref[2 * (first % 8) + first // 8, which] = rows[:half]
    ref[2 * (second % 8) + second // 8, which] = rows[half:]


def stacked(ref, which):
    return jnp.concatenate([ref[i, which] for i in range(ref.shape[0])], axis=0)


def put_stacked(ref, which, rows):
    for i in range(ref.shape[0]):
        ref[i, which] = rows[TILE * i : TILE * (i + 1)]


def factor(mats, count):
    lane = lax.broadcasted_iota(jnp.int32, (TILE, DIM), 1)
    row = lax.broadcasted_iota(jnp.int32, (TILE, DIM), 0)

    def panel(step, start):
        base = pl.multiple_of(step * TILE, TILE)
        rel = lane - base
        inside = (rel >= 0) & (rel < TILE)
        after = rel >= TILE
        unit = jnp.where(rel == row, 1.0, 0.0).astype(F32)
        rows = [mats[n, pl.ds(base, TILE), :] for n in range(count)]
        cols = [
            [jnp.take_along_axis(rows[n], jnp.full((TILE, DIM), 0, jnp.int32) + (base + j), axis=1) for j in range(TILE)]
            for n in range(count)
        ]
        rows = [jnp.where(inside, unit, r) for r in rows]
        for k in range(TILE):
            for n in range(count):
                col = cols[n]
                scale = lax.rsqrt(jnp.broadcast_to(col[k][k : k + 1], (TILE, DIM)))
                pivot = jnp.broadcast_to(rows[n][k : k + 1], (TILE, DIM)) * scale
                mult = jnp.where(row > k, col[k] * scale, 0.0)
                rows[n] = jnp.where(row == k, pivot, rows[n] - mult * pivot)
                for j in range(k + 1, TILE):
                    col[j] = col[j] - mult * (jnp.broadcast_to(col[j][k : k + 1], (TILE, DIM)) * scale)
        for n in range(count):
            high, mid, low = thirds(rows[n])
            none = jnp.zeros_like(rows[n])
            lh = jnp.where(after, high.astype(F32), none)
            lm = jnp.where(after, mid.astype(F32), none)
            ll = jnp.where(after, low.astype(F32), none)
            rh, rm, rl = high.astype(F32), mid.astype(F32), low.astype(F32)
            left = jnp.concatenate([lh, lh, lm, lm, lh, ll], axis=0).astype(BF16)
            right = jnp.concatenate([rh, rm, rh, rm, rl, rh], axis=0).astype(BF16)
            left = left[:, start:]
            change = lax.dot_general(
                left, right, (((0,), (0,)), ((), ())), preferred_element_type=F32
            )
            old = mats[n, start:, :]
            keep = jnp.concatenate([inside] * ((DIM - start) // TILE), axis=0)
            mats[n, start:, :] = jnp.where(keep, 0.0, old) - change
            mats[n, pl.ds(base, TILE), :] = rows[n]

    def run(step, carry):
        panel(step, 0)
        return carry

    lax.fori_loop(0, DIM // TILE, run, 0)


def totals_kernel(own_ref, total_ref):
    gram = jnp.zeros((DIM, DIM), F32)
    state = jnp.zeros((DIM, DIM), F32)
    for n in range(8):
        k = owned_rows(own_ref, n, 1)
        v = owned_rows(own_ref, n, 2)
        gram = gram + contract([(k, k)], 0, 0)
        state = state + contract([(v, k)], 0, 0)
    put_stacked(total_ref, 0, gram)
    put_stacked(total_ref, 1, state)


def scan_kernel(part_ref, out_ref, *, reverse):
    count = part_ref.shape[0]
    order = range(count - 1, -1, -1) if reverse else range(count)
    total = jnp.zeros(part_ref.shape[1:], F32)
    for i in order:
        out_ref[i] = total
        total = total + part_ref[i]


def main_kernel(
    own_ref, before_ref, reg_ref, early_ref, dk_ref, dv_ref, dgram_ref, dstate_ref, total_ref,
    mats, state_in, inverse, key_inv,
):
    wide = lax.broadcasted_iota(jnp.int32, (DIM, DIM), 1)
    tall = lax.broadcasted_iota(jnp.int32, (DIM, DIM), 0)
    lower = tall >= wide
    causal2 = jnp.concatenate([lower, lower], axis=0)
    gram = jnp.where(tall == wide, jnp.broadcast_to(reg_ref[...], (DIM, DIM)), 0.0) + stacked(before_ref, 0)
    state = stacked(before_ref, 1)
    for n in range(8):
        mats[n] = gram
        state_in[n] = state
        if n < 7:
            k = owned_rows(own_ref, n, 1)
            v = owned_rows(own_ref, n, 2)
            gram = gram + contract([(k, k)], 0, 0)
            state = state + contract([(v, k)], 0, 0)
    factor(mats, 8)

    def middle(n):
        low = halves(jnp.where(lower, mats[n], 0.0))
        inv = contract(cross(low, low), 0, 0)
        inv = halves(inv)
        inverse[n, 0] = inv[0]
        inverse[n, 1] = inv[1]
        k = owned_rows(own_ref, n, 1)
        ki = halves(contract([(k, inv[0]), (k, inv[1])], 1, 0))
        key_inv[n, 0] = ki[0]
        key_inv[n, 1] = ki[1]
        mats[n] = contract([(ki[0], k), (ki[1], k)], 1, 1) + jnp.where(tall == wide, 1.0, 0.0)

    def middle_two(i, carry):
        middle(2 * i)
        middle(2 * i + 1)
        return carry

    lax.fori_loop(0, 4, middle_two, 0)
    factor(mats, 8)

    def solve(n):
        q = owned_rows(own_ref, n, 0)
        k = owned_rows(own_ref, n, 1)
        v = owned_rows(own_ref, n, 2)
        g = owned_rows(own_ref, n, 3)
        st = halves(state_in[n])
        inv = (inverse[n, 0], inverse[n, 1])
        ki = (key_inv[n, 0], key_inv[n, 1])
        low = halves(jnp.where(lower, mats[n], 0.0))
        ds = jnp.where(lower, contract([(g, v)], 1, 1), 0.0)
        dsh = halves(ds)
        du = contract([(g, st[0]), (g, st[1]), (dsh[0], k), (dsh[1], k)], 1, 0)
        duh = halves(du)
        rhs = (
            jnp.concatenate([q, duh[0]], axis=0),
            jnp.concatenate([jnp.zeros_like(q), duh[1]], axis=0),
        )
        r = halves(contract(cross(rhs, ki), 1, 1))
        y = halves(jnp.where(causal2, contract(cross(r, low), 1, 1), 0.0))
        x = halves(-contract(cross(y, low), 1, 0))
        uz = contract(cross(rhs, inv) + cross(x, ki), 1, 0)
        uzh = halves(uz)
        ss = jnp.where(causal2, contract([(uzh[0], k), (uzh[1], k)], 1, 1), 0.0)
        u = (uzh[0][:BLOCK], uzh[1][:BLOCK])
        z = (uzh[0][BLOCK:], uzh[1][BLOCK:])
        s = halves(ss[:BLOCK])
        out = contract(cross(u, st), 1, 1) + contract([(s[0], v), (s[1], v)], 1, 0)
        put_rows(early_ref, n, 0, out.astype(BF16))
        put_rows(early_ref, n, 1, uz[BLOCK:].astype(BF16))
        e = halves(ds - ss[BLOCK:])
        neg = (-s[0], -s[1])
        dk_ref[n] = contract(cross(e, u) + cross(neg, z), 0, 0)
        dv_ref[n] = contract([(s[0], g), (s[1], g)], 0, 0)
        dstate = contract([(g, u[0]), (g, u[1])], 0, 0)
        dgram = -contract(cross(z, u), 0, 0)
        dgram_ref[n] = dgram
        dstate_ref[n] = dstate
        return dgram, dstate

    def solve_two(i, carry):
        a = solve(2 * i)
        b = solve(2 * i + 1)
        return carry[0] + (a[0] + b[0]), carry[1] + (a[1] + b[1])

    zero = jnp.zeros((DIM, DIM), F32)
    sums = lax.fori_loop(0, 4, solve_two, (zero, zero))
    put_stacked(total_ref, 0, sums[0])
    put_stacked(total_ref, 1, sums[1])


def final_kernel(own_ref, after_ref, dk_ref, dv_ref, dgram_ref, dstate_ref, late_ref):
    gram = stacked(after_ref, 0)
    state = stacked(after_ref, 1)
    for n in range(7, -1, -1):
        k = owned_rows(own_ref, n, 1)
        v = owned_rows(own_ref, n, 2)
        sym = halves(gram + gram.T)
        st = halves(state)
        dk = dk_ref[n] + contract([(k, sym[0]), (k, sym[1]), (v, st[0]), (v, st[1])], 1, 0)
        dv = dv_ref[n] + contract([(k, st[0]), (k, st[1])], 1, 1)
        put_rows(late_ref, n, 0, dk.astype(BF16))
        put_rows(late_ref, n, 1, dv.astype(BF16))
        if n > 0:
            gram = gram + dgram_ref[n]
            state = state + dstate_ref[n]


def local_totals(own):
    return pl.pallas_call(
        totals_kernel,
        out_shape=jax.ShapeDtypeStruct((16, 2, TILE, DIM), F32),
        compiler_params=PARAMS,
        name="totals",
    )(own)


def scan_parts(parts, reverse):
    def body(part_ref, out_ref):
        scan_kernel(part_ref, out_ref, reverse=reverse)

    return pl.pallas_call(
        body, out_shape=jax.ShapeDtypeStruct(parts.shape, F32), name="scan_rev" if reverse else "scan_fwd"
    )(parts)


def main_part(own, before, reg):
    full = jax.ShapeDtypeStruct((8, DIM, DIM), F32)
    return pl.pallas_call(
        main_kernel,
        out_shape=(
            jax.ShapeDtypeStruct((16, 2, BLOCK // 2, DIM), BF16),
            full, full, full, full,
            jax.ShapeDtypeStruct((16, 2, TILE, DIM), F32),
        ),
        scratch_shapes=[
            pltpu.VMEM((8, DIM, DIM), F32),
            pltpu.VMEM((8, DIM, DIM), F32),
            pltpu.VMEM((8, 2, DIM, DIM), BF16),
            pltpu.VMEM((8, 2, DIM, DIM), BF16),
        ],
        compiler_params=PARAMS,
        name="main",
    )(own, before, reg)


def final_part(own, after, dk, dv, dgram, dstate):
    return pl.pallas_call(
        final_kernel,
        out_shape=jax.ShapeDtypeStruct((16, 2, BLOCK // 2, DIM), BF16),
        compiler_params=PARAMS,
        name="final",
    )(own, after, dk, dv, dgram, dstate)


AXES = ("seq", "head")
TOKEN_GROUPS = [[(2 * m + h % 2) * 8 + h // 2 for h in range(16)] for m in range(16)]
SCAN_GROUPS = [[16 * m + r for m in range(16)] for r in range(16)]


def swap(array, groups):
    return lax.all_to_all(array, AXES, 0, 0, axis_index_groups=groups)


def carried(total, reverse):
    return swap(scan_parts(swap(total, SCAN_GROUPS), reverse), SCAN_GROUPS)


def on_device(queries, keys, values, out_grad, regular):
    own = swap(jnp.stack([queries, keys, values, out_grad], axis=1), TOKEN_GROUPS)
    reg = lax.dynamic_slice_in_dim(regular, lax.axis_index("seq") % 2, 1, 0)
    before = carried(local_totals(own), False)
    early, dk, dv, dgram, dstate, total = main_part(own, before, reg)
    after = carried(total, True)
    late = final_part(own, after, dk, dv, dgram, dstate)
    back = swap(jnp.concatenate([early, late], axis=1), TOKEN_GROUPS)
    return back[:, 0], back[:, 1], back[:, 2], back[:, 3]


def solution(mesh):
    placed = P(None, ("seq", "head"), None)
    return jax.shard_map(
        on_device,
        mesh=mesh,
        in_specs=(placed, placed, placed, placed, P("head", None)),
        out_specs=(placed, placed, placed, placed),
        check_vma=False,
    )
```

```python
import jax
import jax.numpy as jnp
from jax import lax
from jax.experimental import pallas as pl
from jax.experimental.pallas import tpu as pltpu
from jax.sharding import PartitionSpec as P

F32 = jnp.float32
BF16 = jnp.bfloat16
BLOCK = 128
DIM = 128
TILE = 8
PARAMS = pltpu.CompilerParams(vmem_limit_bytes=56 * 1024 * 1024)


def halves(x):
    high = x.astype(BF16)
    return high, (x - high.astype(F32)).astype(BF16)


def thirds(x):
    high = x.astype(BF16)
    rest = x - high.astype(F32)
    mid = rest.astype(BF16)
    return high, mid, (rest - mid.astype(F32)).astype(BF16)


def contract(pairs, left_dim, right_dim):
    left = [a for a, _ in pairs]
    right = [b for _, b in pairs]
    left = left[0] if len(left) == 1 else jnp.concatenate(left, axis=left_dim)
    right = right[0] if len(right) == 1 else jnp.concatenate(right, axis=right_dim)
    return lax.dot_general(
        left, right, (((left_dim,), (right_dim,)), ((), ())), preferred_element_type=F32
    )


def cross(left, right):
    return [(left[0], right[0]), (left[0], right[1]), (left[1], right[0])]


def place_of(chunk, side):
    return 2 * (chunk % 8) + jnp.bitwise_xor(chunk // 8, side)


def owned_rows(ref, block, which, side):
    first = place_of(2 * block, side)
    second = place_of(2 * block + 1, side)
    return jnp.concatenate([ref[first, which], ref[second, which]], axis=0)


def put_rows(ref, block, which, rows, side):
    half = BLOCK // 2
    ref[place_of(2 * block, side), which] = rows[:half]
    ref[place_of(2 * block + 1, side), which] = rows[half:]


def together(steps):
    done = [None] * len(steps)
    live = list(range(len(steps)))
    while live:
        for i in list(live):
            try:
                next(steps[i])
            except StopIteration as end:
                done[i] = end.value
                live.remove(i)
    return done


def factor(mats, count):
    lane = lax.broadcasted_iota(jnp.int32, (TILE, DIM), 1)
    row = lax.broadcasted_iota(jnp.int32, (TILE, DIM), 0)

    def panel(step, start):
        base = pl.multiple_of(step * TILE, TILE)
        rel = lane - base
        inside = (rel >= 0) & (rel < TILE)
        after = rel >= TILE
        unit = jnp.where(rel == row, 1.0, 0.0).astype(F32)
        rows = [mats[n, pl.ds(base, TILE), :] for n in range(count)]
        cols = [
            [jnp.take_along_axis(rows[n], jnp.full((TILE, DIM), 0, jnp.int32) + (base + j), axis=1) for j in range(TILE)]
            for n in range(count)
        ]
        rows = [jnp.where(inside, unit, r) for r in rows]
        for k in range(TILE):
            for n in range(count):
                col = cols[n]
                scale = lax.rsqrt(jnp.broadcast_to(col[k][k : k + 1], (TILE, DIM)))
                pivot = jnp.broadcast_to(rows[n][k : k + 1], (TILE, DIM)) * scale
                mult = jnp.where(row > k, col[k] * scale, 0.0)
                rows[n] = jnp.where(row == k, pivot, rows[n] - mult * pivot)
                for j in range(k + 1, TILE):
                    col[j] = col[j] - mult * jnp.broadcast_to(mult[j : j + 1], (TILE, DIM))
        for n in range(count):
            high, mid, low = thirds(rows[n])
            none = jnp.zeros_like(rows[n])
            lh = jnp.where(after, high.astype(F32), none)
            lm = jnp.where(after, mid.astype(F32), none)
            ll = jnp.where(after, low.astype(F32), none)
            rh, rm, rl = high.astype(F32), mid.astype(F32), low.astype(F32)
            left = jnp.concatenate([lh, lh, lm, lm, lh, ll], axis=0).astype(BF16)
            right = jnp.concatenate([rh, rm, rh, rm, rl, rh], axis=0).astype(BF16)
            left = left[:, start:]
            change = lax.dot_general(
                left, right, (((0,), (0,)), ((), ())), preferred_element_type=F32
            )
            old = mats[n, start:, :]
            keep = jnp.concatenate([inside] * ((DIM - start) // TILE), axis=0)
            mats[n, start:, :] = jnp.where(keep, 0.0, old) - change
            mats[n, pl.ds(base, TILE), :] = rows[n]

    def run(step, carry):
        panel(step, 0)
        return carry

    lax.fori_loop(0, DIM // TILE, run, 0)


def totals_kernel(side_ref, kv_ref, total_ref):
    side = side_ref[0]
    gram = jnp.zeros((DIM, DIM), F32)
    state = jnp.zeros((DIM, DIM), F32)
    for n in range(8):
        k = owned_rows(kv_ref, n, 0, side)
        v = owned_rows(kv_ref, n, 1, side)
        gram = gram + contract([(k, k)], 0, 0)
        state = state + contract([(v, k)], 0, 0)
    total_ref[:DIM] = gram
    total_ref[DIM:] = state


def factor_kernel(side_ref, kv_ref, before_ref, reg_ref, low_ref, inverse, key_inv, mats):
    side = side_ref[0]
    wide = lax.broadcasted_iota(jnp.int32, (DIM, DIM), 1)
    tall = lax.broadcasted_iota(jnp.int32, (DIM, DIM), 0)
    lower = tall >= wide
    gram = before_ref[:DIM] + jnp.where(tall == wide, jnp.broadcast_to(reg_ref[...], (DIM, DIM)), 0.0)
    for n in range(8):
        mats[n] = gram
        if n < 7:
            k = owned_rows(kv_ref, n, 0, side)
            gram = gram + contract([(k, k)], 0, 0)
    factor(mats, 8)

    def middle(n):
        low = halves(jnp.where(lower, mats[n], 0.0))
        yield
        inv = halves(contract(cross(low, low), 0, 0))
        yield
        inverse[n, 0] = inv[0]
        inverse[n, 1] = inv[1]
        k = owned_rows(kv_ref, n, 0, side)
        ki = halves(contract([(k, inv[0]), (k, inv[1])], 1, 0))
        yield
        key_inv[n, 0] = ki[0]
        key_inv[n, 1] = ki[1]
        mats[n] = contract([(ki[0], k), (ki[1], k)], 1, 1) + jnp.where(tall == wide, 1.0, 0.0)

    together([middle(j) for j in range(8)])
    factor(mats, 8)
    for n in range(8):
        low = halves(jnp.where(lower, mats[n], 0.0))
        low_ref[n, 0] = low[0]
        low_ref[n, 1] = low[1]


def solve_kernel(
    side_ref, qg_ref, kv_ref, before_ref, low_ref, inverse, key_inv,
    early_ref, dk_ref, dv_ref, dgram_ref, dstate_ref, total_ref, state_in,
):
    side = side_ref[0]
    wide = lax.broadcasted_iota(jnp.int32, (DIM, DIM), 1)
    tall = lax.broadcasted_iota(jnp.int32, (DIM, DIM), 0)
    lower = tall >= wide
    causal2 = jnp.concatenate([lower, lower], axis=0)
    state = before_ref[DIM:]
    for n in range(8):
        state_in[n] = state
        if n < 7:
            k = owned_rows(kv_ref, n, 0, side)
            v = owned_rows(kv_ref, n, 1, side)
            state = state + contract([(v, k)], 0, 0)

    def solve(n):
        q = owned_rows(qg_ref, n, 0, side)
        g = owned_rows(qg_ref, n, 1, side)
        k = owned_rows(kv_ref, n, 0, side)
        v = owned_rows(kv_ref, n, 1, side)
        st = halves(state_in[n])
        inv = (inverse[n, 0], inverse[n, 1])
        ki = (key_inv[n, 0], key_inv[n, 1])
        low = (low_ref[n, 0], low_ref[n, 1])
        ds = jnp.where(lower, contract([(g, v)], 1, 1), 0.0)
        dsh = halves(ds)
        yield
        du = contract([(g, st[0]), (g, st[1]), (dsh[0], k), (dsh[1], k)], 1, 0)
        duh = halves(du)
        yield
        rhs = (
            jnp.concatenate([q, duh[0]], axis=0),
            jnp.concatenate([jnp.zeros_like(q), duh[1]], axis=0),
        )
        r = halves(contract(cross(rhs, ki), 1, 1))
        yield
        y = halves(jnp.where(causal2, contract(cross(r, low), 1, 1), 0.0))
        yield
        x = halves(-contract(cross(y, low), 1, 0))
        yield
        uz = contract(cross(rhs, inv) + cross(x, ki), 1, 0)
        uzh = halves(uz)
        yield
        ss = jnp.where(causal2, contract([(uzh[0], k), (uzh[1], k)], 1, 1), 0.0)
        u = (uzh[0][:BLOCK], uzh[1][:BLOCK])
        z = (uzh[0][BLOCK:], uzh[1][BLOCK:])
        s = halves(ss[:BLOCK])
        yield
        out = contract(cross(u, st), 1, 1) + contract([(s[0], v), (s[1], v)], 1, 0)
        yield
        put_rows(early_ref, n, 0, out.astype(BF16), side)
        put_rows(early_ref, n, 1, uz[BLOCK:].astype(BF16), side)
        e = halves(ds - ss[BLOCK:])
        yield
        neg = (-s[0], -s[1])
        dk_ref[n] = contract(cross(e, u) + cross(neg, z), 0, 0)
        dv_ref[n] = contract([(s[0], g), (s[1], g)], 0, 0)
        yield
        dstate = contract([(g, u[0]), (g, u[1])], 0, 0)
        yield
        dgram = -contract(cross(z, u), 0, 0)
        dgram_ref[n] = dgram
        dstate_ref[n] = dstate
        return dgram, dstate

    def solve_some(i, carry):
        done = together([solve(8 * i + j) for j in range(8)])
        return (
            carry[0] + sum(a for a, _ in done),
            carry[1] + sum(b for _, b in done),
        )

    zero = jnp.zeros((DIM, DIM), F32)
    sums = lax.fori_loop(0, 1, solve_some, (zero, zero)) if 8 < 8 else solve_some(0, (zero, zero))
    total_ref[:DIM] = sums[0]
    total_ref[DIM:] = sums[1]


def final_kernel(side_ref, kv_ref, after_ref, dk_ref, dv_ref, dgram_ref, dstate_ref, late_ref):
    side = side_ref[0]
    gram = after_ref[:DIM]
    state = after_ref[DIM:]
    later = [None] * 8
    for n in range(7, -1, -1):
        later[n] = (gram, state)
        if n > 0:
            gram = gram + dgram_ref[n]
            state = state + dstate_ref[n]

    def finish(n):
        k = owned_rows(kv_ref, n, 0, side)
        v = owned_rows(kv_ref, n, 1, side)
        sym = halves(later[n][0] + later[n][0].T)
        st = halves(later[n][1])
        yield
        dk = dk_ref[n] + contract([(k, sym[0]), (k, sym[1]), (v, st[0]), (v, st[1])], 1, 0)
        dv = dv_ref[n] + contract([(k, st[0]), (k, st[1])], 1, 1)
        yield
        put_rows(late_ref, n, 0, dk.astype(BF16), side)
        put_rows(late_ref, n, 1, dv.astype(BF16), side)

    together([finish(n) for n in range(8)])


SCALAR = pl.BlockSpec(memory_space=pltpu.SMEM)
VECTOR = pl.BlockSpec(memory_space=pltpu.VMEM)
SQUARE = jax.ShapeDtypeStruct((DIM, DIM), F32)
SQUARES = jax.ShapeDtypeStruct((8, DIM, DIM), F32)
SPLIT = jax.ShapeDtypeStruct((8, 2, DIM, DIM), BF16)
TOKENS = jax.ShapeDtypeStruct((16, 2, BLOCK // 2, DIM), BF16)


def local(kernel, name, outs, count, scratch=()):
    return pl.pallas_call(
        kernel,
        out_shape=outs,
        in_specs=[SCALAR] + [VECTOR] * (count - 1),
        scratch_shapes=list(scratch),
        compiler_params=PARAMS,
        name=name,
    )


AXES = ("seq", "head")


def owner(z, side, head):
    x = head % 2 if side == 0 else 3 - head % 2
    return 32 * z + 8 * x + head // 2


TOKEN_GROUPS = [[owner(z, side, h) for h in range(16)] for z in range(8) for side in range(2)]


def swap(array):
    return lax.all_to_all(array, AXES, 0, 0, axis_index_groups=TOKEN_GROUPS)


def move(array, flip_z, flip_side, keep=None):
    pairs = [
        (owner(z, side, h), owner(z ^ flip_z, side ^ flip_side, h))
        for z in range(8)
        for side in range(2)
        for h in range(16)
        if keep is None or keep(z)
    ]
    return lax.ppermute(array, AXES, pairs)


def carried(part, z, side, reverse):
    def beyond(bit):
        return (bit == 0 if reverse else bit == 1).astype(F32)

    across = move(part, 0, 1)
    along = move(part, 1, 0)
    both = move(part, 1, 1)
    total = (part + across) + (along + both)
    ahead = beyond(side) * across + beyond(z % 2) * (along + both)
    other = move(total, 2, 0)
    ahead = ahead + beyond(z // 2 % 2) * other
    total = total + other
    far = move(total, 7, 0, (lambda z: z >= 4) if reverse else (lambda z: z < 4))
    return ahead + far


def on_device(queries, keys, values, out_grad, regular):
    place = lax.axis_index("seq")
    z = place // 4
    x = place % 4
    side = x // 2
    sides = side.reshape(1).astype(jnp.int32)
    kv = swap(jnp.stack([keys, values], axis=1))
    qg = swap(jnp.stack([queries, out_grad], axis=1))
    reg = lax.dynamic_slice_in_dim(regular, (x % 2) ^ side, 1, 0)
    pair = jax.ShapeDtypeStruct((2 * DIM, DIM), F32)
    gram_before = carried(local(totals_kernel, "totals", pair, 2)(sides, kv), z, side, False)
    state_before = gram_before
    low, inverse, key_inv = local(
        factor_kernel, "factor", (SPLIT, SPLIT, SPLIT), 4, [pltpu.VMEM((8, DIM, DIM), F32)]
    )(sides, kv, gram_before, reg)
    early, dk, dv, dgram, dstate, total = local(
        solve_kernel,
        "solve",
        (TOKENS, SQUARES, SQUARES, SQUARES, SQUARES, jax.ShapeDtypeStruct((2 * DIM, DIM), F32)),
        7,
        [pltpu.VMEM((8, DIM, DIM), F32)],
    )(sides, qg, kv, state_before, low, inverse, key_inv)
    after = carried(total, z, side, True)
    late = local(final_kernel, "final", TOKENS, 7)(sides, kv, after, dk, dv, dgram, dstate)
    early = swap(early)
    late = swap(late)
    return early[:, 0], early[:, 1], late[:, 0], late[:, 1]


def solution(mesh):
    placed = P(None, ("seq", "head"), None)
    return jax.shard_map(
        on_device,
        mesh=mesh,
        in_specs=(placed, placed, placed, placed, P("head", None)),
        out_specs=(placed, placed, placed, placed),
        check_vma=False,
    )
```
